32 devices in a mesh: va: 8 (over z, y), vb: 4 (over x, core).
Axes of the slice: x: 2, y: 2, z: 4, core: 2. Of those that a mesh axis runs over, the one named last changes fastest.
Arguments:
- amplitudes: bfloat16 [2, 2, 2048, 2048], P(None, None, 'va', 'vb'), may hold values from -6 to 6
- integrals: bfloat16 [4, 2048, 2048], P(None, 'va', 'vb'), may hold values from -0.125 to 0.125
- occ_energy: float32 [2], replicated, may hold values from -2 to -0.5
- vir_energy: float32 [2048], replicated, may hold values from 0.2 to 3
- screen: int32 [8, 8], replicated, may hold values from -1 to 15, as said below
- lengths: int32 [8], replicated, may hold values from 2 to 8, as said below
Outputs:
- update: float32 [2, 2, 2048, 2048], P(None, None, 'va', 'vb')
The draws below stay inside these ranges and needn't reach their ends.
Inputs may be any that keep to these rules, and one draw needn't show every extreme that they name: `screen`: row r holds lengths[r] distinct tile numbers below 16 in its first slots and -1 in the others. `lengths`: exactly one grid row lists 8 tiles; every other row lists at most 4.
All inputs are finite; a program needn't handle non-finite values.
Results may differ from the reference program's by a relative error of at most 0.0031.
Values may be sent and summed in bfloat16 or wider, within the bound.
A program may use at most 64 MiB of HBM per device.

```python
import jax
import jax.numpy as jnp
from jax import lax

V = 2048
TILE = 128
OCC = 2
LIST = 8
TILES = 16
N_VA = 8


def screened_rows(key):
    base = jax.random.fold_in(key, 7)
    key_len, key_row, key_perm = jax.random.split(base, 3)
    row_lens = jax.random.randint(key_len, (N_VA,), 2, LIST // 2 + 1)
    full_row = jax.random.randint(key_row, (), 0, N_VA)
    row_lens = jnp.where(jnp.arange(N_VA) == full_row, LIST, row_lens).astype(jnp.int32)
    row_keys = jax.random.split(key_perm, N_VA)
    shuffled = jax.vmap(lambda one_key: jax.random.permutation(one_key, TILES))(row_keys)[:, :LIST]
    tile_ids = jnp.where(jnp.arange(LIST)[None, :] < row_lens[:, None], shuffled, -1).astype(jnp.int32)
    return (tile_ids, row_lens)


def draw_screen(key, part):
    return screened_rows(key)[0]


def draw_lengths(key, part):
    return screened_rows(key)[1]


def block_scale(own_key, dims, pieces, low, largest):
    def one(position, blocks):
        steps = jax.random.uniform(jax.random.fold_in(jax.random.fold_in(own_key, 6), position), (blocks,), jnp.float32, low / len(pieces), largest / len(pieces))
        return jnp.repeat(jnp.exp(steps), dims[position] // blocks).reshape((-1,) + (1,) * (len(dims) - position - 1))

    factor_of = one(*pieces[0])
    for cut in pieces[1:]:
        factor_of = factor_of * one(*cut)
    return factor_of


def noise(rng, dims, scale, most, pieces=(), kind=jnp.bfloat16):
    result = scale * jax.random.normal(rng, dims, jnp.float32)
    if pieces:
        result = result * block_scale(rng, dims, pieces, -0.22, 0.18)
    return jnp.clip(result, -most, most).astype(kind)


def setup_inputs(seed: int = 0) -> dict:
    key_of = jax.random.split(jax.random.key(seed), 7)
    amplitudes = noise(key_of[0], (OCC, OCC, V, V), 1.0, 6.0, ((2, 8), (3, 4)))
    integrals = noise(key_of[1], (OCC * OCC, V, V), (OCC * LIST * TILE) ** -0.5, 0.125, ((1, 8), (2, 4)))
    occ_energy = jnp.clip(jax.random.uniform(key_of[2], (OCC,), jnp.float32, -2.0, -0.5), -2.0, -0.5)
    vir_energy = jnp.clip(jax.random.uniform(key_of[3], (V,), jnp.float32, 0.2, 3.0), 0.2, 3.0)
    screen = draw_screen(jax.random.fold_in(key_of[6], 71), 0)
    lengths = draw_lengths(jax.random.fold_in(key_of[6], 71), 0)
    return dict(amplitudes=amplitudes, integrals=integrals, occ_energy=occ_energy, vir_energy=vir_energy, screen=screen, lengths=lengths)


def reference(amplitudes, integrals, occ_energy, vir_energy, screen, lengths):
    row_len = V // N_VA
    slots = screen.shape[1]
    offsets = jnp.arange(TILE, dtype=jnp.int32)
    blocks = integrals.reshape(OCC, OCC, V, V)

    def row_term(grid_row):
        begin_at = (grid_row * row_len).astype(jnp.int32)
        own_rows = lax.dynamic_slice_in_dim(amplitudes, begin_at, row_len, 2).astype(jnp.float32)
        mirror = jnp.swapaxes(lax.dynamic_slice_in_dim(amplitudes, begin_at, row_len, 3), 2, 3).astype(jnp.float32)
        spin_amp = (2.0 * own_rows - mirror).astype(jnp.bfloat16)
        tile_ids = jnp.maximum(screen[grid_row], 0).astype(jnp.int32)
        is_live = jnp.arange(slots, dtype=jnp.int32) < lengths[grid_row]
        columns = (tile_ids[:, None] * TILE + offsets[None, :]).reshape(-1).astype(jnp.int32)
        picked = jnp.take(spin_amp, columns, axis=3).astype(jnp.float32)
        k_rows = jnp.take(blocks, columns, axis=2).astype(jnp.float32)
        keep_cols = jnp.repeat(is_live, TILE).astype(jnp.float32)
        k_rows = k_rows * keep_cols[None, None, :, None]
        return jnp.einsum("ikac,kjcb->ijab", picked, k_rows, precision=lax.Precision.HIGHEST)

    cycle = lax.map(row_term, jnp.arange(N_VA, dtype=jnp.int32))
    cycle = jnp.transpose(cycle, (1, 2, 0, 3, 4)).reshape(OCC, OCC, V, V)
    denominator = (occ_energy[:, None, None, None] + occ_energy[None, :, None, None]
                   - vir_energy[None, None, :, None] - vir_energy[None, None, None, :])
    return cycle / denominator
```

```python
import functools

import jax
import jax.numpy as jnp
from jax import lax
from jax.experimental import pallas as pl
from jax.experimental.pallas import tpu as pltpu
from jax.sharding import PartitionSpec as P

TILE = 128
PAIR = 2
MESH = pl.DeviceIdType.MESH


def gather_kernel(
    count_va, count_vb, amp_ref, turned_ref, int_ref, whole_k, spin_all,
    landed, spin, z_send, z_recv, y_send, y_recv, m_send, m_recv, s_send, s_recv, own_sem,
):
    va = lax.axis_index("va")
    vb = lax.axis_index("vb")
    ratio = count_va // count_vb
    lines = count_va // PAIR
    outers = count_vb // PAIR
    line, side = va // PAIR, va % PAIR
    outer, core = vb // PAIR, vb % PAIR
    chunks, rows, _ = int_ref.shape
    row_len = amp_ref.shape[2]

    def k_slot(owner, chunk):
        return whole_k.at[chunk, pl.ds(pl.multiple_of(owner * rows, rows), rows)]

    def remote(src, dst, send, recv, target):
        return pltpu.make_async_remote_copy(
            src_ref=src, dst_ref=dst, send_sem=send, recv_sem=recv, device_id=target, device_id_type=MESH
        )

    def mirror_copy(part):
        return remote(
            turned_ref.at[part], landed.at[va % ratio], m_send.at[part], m_recv.at[va % ratio],
            {"va": vb * ratio + part, "vb": va // ratio},
        )

    def mirror_arrival(part):
        return remote(
            turned_ref.at[part], landed.at[part], m_send.at[part], m_recv.at[part],
            {"va": vb * ratio + part, "vb": va // ratio},
        )

    def mirror_own(part):
        return pltpu.make_async_copy(turned_ref.at[part], landed.at[part], m_recv.at[part])

    for part in range(ratio):
        is_own = va == vb * ratio + part

        @pl.when(is_own)
        def _():
            mirror_own(part).start()

        @pl.when(jnp.logical_not(is_own))
        def _():
            mirror_copy(part).start()

    def source(direction, step):
        return line - step if direction == 0 else line + step

    def block_at(direction, step, chunk):
        if step == 0:
            return int_ref.at[chunk]
        return k_slot(source(direction, step) * PAIR + side, chunk)

    def line_send(direction, step, chunk):
        to = line + 1 if direction == 0 else line - 1
        return remote(
            block_at(direction, step, chunk),
            k_slot(source(direction, step) * PAIR + side, chunk),
            z_send.at[direction, step, chunk],
            z_recv.at[direction, step, chunk],
            {"va": to * PAIR + side},
        )

    def line_arrival(direction, step, chunk):
        here = k_slot(source(direction, step) * PAIR + side, chunk)
        return remote(
            here, here, z_send.at[direction, step - 1, chunk], z_recv.at[direction, step - 1, chunk],
            {"va": va},
        )

    def may_send(direction, step):
        if direction == 0:
            return jnp.logical_and(line - step >= 0, line + 1 < lines)
        return jnp.logical_and(line + step < lines, line - 1 >= 0)

    def has_arrival(direction, step):
        return line - step >= 0 if direction == 0 else line + step < lines

    def side_send(direction, step, chunk):
        return remote(
            block_at(direction, step, chunk),
            k_slot(source(direction, step) * PAIR + side, chunk),
            y_send.at[direction, step, chunk],
            y_recv.at[direction, step, chunk],
            {"va": line * PAIR + 1 - side},
        )

    def side_arrival(direction, step, chunk):
        here = k_slot(source(direction, step) * PAIR + 1 - side, chunk)
        return remote(
            here, here, y_send.at[direction, step, chunk], y_recv.at[direction, step, chunk], {"va": va}
        )

    def own_copy(chunk):
        return pltpu.make_async_copy(int_ref.at[chunk], k_slot(va, chunk), own_sem.at[chunk])

    for chunk in range(chunks):
        for direction in range(2):

            @pl.when(may_send(direction, 0))
            def _():
                line_send(direction, 0, chunk).start()

        side_send(0, 0, chunk).start()
    for chunk in range(chunks):
        own_copy(chunk).start()

    def line_step(step):
        for chunk in range(chunks):
            for direction in range(2):

                @pl.when(has_arrival(direction, step))
                def _():
                    line_arrival(direction, step, chunk).wait_recv()

                    @pl.when(may_send(direction, step))
                    def _():
                        line_send(direction, step, chunk).start()

                    side_send(direction, step, chunk).start()

    def spin_send(shift):
        to = lax.rem(outer + shift, outers)
        return remote(
            spin, spin_all.at[vb], s_send.at[0, shift], s_recv.at[0, shift], {"vb": to * PAIR + core}
        )

    def spin_arrival(shift):
        here = spin_all.at[lax.rem(outer + outers - shift, outers) * PAIR + core]
        return remote(here, here, s_send.at[0, shift], s_recv.at[0, shift], {"vb": vb})

    def spin_relay(shift):
        held = spin_all.at[lax.rem(outer + outers - shift, outers) * PAIR + core]
        src = spin if shift == 0 else held
        return remote(
            src, held, s_send.at[1, shift], s_recv.at[1, shift], {"vb": outer * PAIR + 1 - core}
        )

    def relay_arrival(shift):
        here = spin_all.at[lax.rem(outer + outers - shift, outers) * PAIR + 1 - core]
        return remote(here, here, s_send.at[1, shift], s_recv.at[1, shift], {"vb": vb})

    def spin_own():
        return pltpu.make_async_copy(spin, spin_all.at[vb], own_sem.at[chunks])

    def spin_step():
        for part in range(ratio):
            is_own = va == vb * ratio + part

            @pl.when(is_own)
            def _():
                mirror_own(part).wait()

            @pl.when(jnp.logical_not(is_own))
            def _():
                mirror_arrival(part).wait_recv()

            cols = slice(part * row_len, (part + 1) * row_len)
            spin[:, :, :, cols] = (
                2.0 * amp_ref[:, :, :, cols].astype(jnp.float32) - landed[part].astype(jnp.float32)
            ).astype(spin.dtype)
        for shift in range(1, outers):
            spin_send(shift).start()
        spin_relay(0).start()
        spin_own().start()

    for step in range(1, lines):
        line_step(step)
        if step == 1:
            spin_step()
    if lines == 1:
        spin_step()
    for shift in range(1, outers):
        spin_arrival(shift).wait_recv()
        spin_relay(shift).start()

    for chunk in range(chunks):
        own_copy(chunk).wait()
        side_arrival(0, 0, chunk).wait_recv()
        side_send(0, 0, chunk).wait_send()
        for direction in range(2):

            @pl.when(may_send(direction, 0))
            def _():
                line_send(direction, 0, chunk).wait_send()

    for step in range(1, lines):
        for chunk in range(chunks):
            for direction in range(2):

                @pl.when(may_send(direction, step))
                def _():
                    line_send(direction, step, chunk).wait_send()

                @pl.when(has_arrival(direction, step))
                def _():
                    side_arrival(direction, step, chunk).wait_recv()
                    side_send(direction, step, chunk).wait_send()

    for part in range(ratio):

        @pl.when(jnp.logical_not(va == vb * ratio + part))
        def _():
            mirror_copy(part).wait_send()

    spin_own().wait()
    for shift in range(outers):
        relay_arrival(shift).wait_recv()
        spin_relay(shift).wait_send()
    for shift in range(1, outers):
        spin_send(shift).wait_send()


def gather_all(amplitudes, turned, integrals, count_va, count_vb):
    occ_a, occ_b, row_len, col_len = amplitudes.shape
    chunks, rows, cols = integrals.shape
    ratio = count_va // count_vb
    lines = count_va // PAIR
    outers = count_vb // PAIR
    dma = pltpu.SemaphoreType.DMA
    return pl.pallas_call(
        functools.partial(gather_kernel, count_va, count_vb),
        out_shape=(
            jax.ShapeDtypeStruct((chunks, count_va * rows, cols), integrals.dtype),
            jax.ShapeDtypeStruct((count_vb, occ_a, occ_b, row_len, col_len), amplitudes.dtype),
        ),
        in_specs=[pl.BlockSpec(memory_space=pltpu.VMEM)] * 3,
        out_specs=(pl.BlockSpec(memory_space=pl.ANY),) * 2,
        scratch_shapes=[
            pltpu.VMEM(turned.shape, turned.dtype),
            pltpu.VMEM(amplitudes.shape, amplitudes.dtype),
            dma((2, lines, chunks)),
            dma((2, lines, chunks)),
            dma((2, lines, chunks)),
            dma((2, lines, chunks)),
            dma((ratio,)),
            dma((ratio,)),
            dma((2, outers)),
            dma((2, outers)),
            dma((chunks + 1,)),
        ],
        compiler_params=pltpu.CompilerParams(has_side_effects=True),
    )(amplitudes, turned, integrals)


def cycle_kernel(per_shard, ids, count, occ, spin_ref, k_ref, rows_ref, cols_ref, out_ref):
    slot = pl.program_id(0)
    occ_count = spin_ref.shape[1]

    @pl.when(slot == 0)
    def _():
        out_ref[...] = jnp.zeros_like(out_ref)

    @pl.when(slot < count[0])
    def _():
        for j in range(occ_count):
            right = jnp.concatenate([k_ref[k * occ_count + j] for k in range(occ_count)], axis=0)
            for i in range(occ_count):
                left = jnp.concatenate([spin_ref[0, i, k] for k in range(occ_count)], axis=1)
                out_ref[i, j] += jnp.dot(left, right, preferred_element_type=jnp.float32)

    @pl.when(slot == pl.num_programs(0) - 1)
    def _():
        for i in range(occ_count):
            for j in range(occ_count):
                bottom = (occ[i] + occ[j] - rows_ref[...]) - cols_ref[...]
                out_ref[i, j] = out_ref[i, j] / bottom


def local(amplitudes, integrals, occ_energy, vir_energy, screen, lengths):
    count_va = lax.axis_size("va")
    count_vb = lax.axis_size("vb")
    occ_a, occ_b, row_len, col_len = amplitudes.shape
    ratio = count_va // count_vb
    cols = integrals.shape[2]
    turned = jnp.transpose(
        amplitudes.reshape(occ_a, occ_b, row_len, ratio, row_len), (3, 0, 1, 4, 2)
    )
    whole_k, spin_all = gather_all(amplitudes, turned, integrals, count_va, count_vb)
    my_row = lax.axis_index("va")
    slots = screen.shape[1]
    per_shard = col_len // TILE
    row_count = lax.dynamic_slice_in_dim(lengths, my_row, 1)
    ids = lax.dynamic_index_in_dim(screen, my_row, 0, keepdims=False)
    ids = jnp.maximum(ids[jnp.minimum(jnp.arange(slots), row_count[0] - 1)], 0)
    vir_rows = lax.dynamic_slice_in_dim(vir_energy, my_row * row_len, row_len)[:, None]
    vir_cols = lax.dynamic_slice_in_dim(vir_energy, lax.axis_index("vb") * cols, cols)[None, :]
    return pl.pallas_call(
        functools.partial(cycle_kernel, per_shard),
        out_shape=jax.ShapeDtypeStruct((occ_a, occ_b, row_len, cols), jnp.float32),
        grid_spec=pltpu.PrefetchScalarGridSpec(
            num_scalar_prefetch=3,
            grid=(slots,),
            in_specs=[
                pl.BlockSpec(
                    (1, occ_a, occ_b, row_len, TILE),
                    lambda m, ids, count, occ: (ids[m] // per_shard, 0, 0, 0, ids[m] % per_shard),
                ),
                pl.BlockSpec((integrals.shape[0], TILE, cols), lambda m, ids, count, occ: (0, ids[m], 0)),
                pl.BlockSpec((row_len, 1), lambda m, ids, count, occ: (0, 0)),
                pl.BlockSpec((1, cols), lambda m, ids, count, occ: (0, 0)),
            ],
            out_specs=pl.BlockSpec(
                (occ_a, occ_b, row_len, cols), lambda m, ids, count, occ: (0, 0, 0, 0)
            ),
        ),
    )(ids, row_count, occ_energy, spin_all, whole_k, vir_rows, vir_cols)


def solution(mesh):
    return jax.shard_map(
        local,
        mesh=mesh,
        in_specs=(P(None, None, "va", "vb"), P(None, "va", "vb"), P(), P(), P(), P()),
        out_specs=P(None, None, "va", "vb"),
        check_vma=False,
    )
```

```python
import functools

import jax
import jax.numpy as jnp
from jax import lax
from jax.experimental import pallas as pl
from jax.experimental.pallas import tpu as pltpu
from jax.sharding import PartitionSpec as P

TILE = 128
PAIR = 2
SPLIT = 2
MESH = pl.DeviceIdType.MESH


def gather_kernel(
    count_va, count_vb, amp_ref, turned_ref, int_ref, whole_k, spin_all,
    landed, passing, spin, z_send, z_recv, y_send, y_recv, m_send, m_recv, x_send, x_recv, s_send, s_recv, own_sem,
):
    va = lax.axis_index("va")
    vb = lax.axis_index("vb")
    ratio = count_va // count_vb
    lines = count_va // PAIR
    outers = count_vb // PAIR
    line, side = va // PAIR, va % PAIR
    outer, core = vb // PAIR, vb % PAIR
    blocks, rows, _ = int_ref.shape
    part_rows = rows // SPLIT
    chunks = blocks * SPLIT
    early = chunks - 1
    halves = amp_ref.shape[0]
    row_len = amp_ref.shape[2]

    def k_slot(owner, chunk):
        begin = owner * rows + chunk % SPLIT * part_rows
        return whole_k.at[chunk // SPLIT, pl.ds(pl.multiple_of(begin, part_rows), part_rows)]

    def own_slot(chunk):
        return int_ref.at[chunk // SPLIT, pl.ds(chunk % SPLIT * part_rows, part_rows)]

    def remote(src, dst, send, recv, target):
        return pltpu.make_async_remote_copy(
            src_ref=src, dst_ref=dst, send_sem=send, recv_sem=recv, device_id=target, device_id_type=MESH
        )

    next_vb = lax.rem(outer + 1, outers) * PAIR + core
    last_vb = lax.rem(outer + outers - 1, outers) * PAIR + core

    def by_relay(half):
        return outers > 1 and half % 2 == 1

    def mirror_own(part):
        return pltpu.make_async_copy(turned_ref.at[part], landed.at[part], own_sem.at[part])

    def mirror_straight(part, half):
        return remote(
            turned_ref.at[part, half], landed.at[va % ratio, half],
            m_send.at[0, part, half], m_recv.at[va % ratio, half],
            {"va": vb * ratio + part, "vb": va // ratio},
        )

    def mirror_out(part, half):
        return remote(
            turned_ref.at[part, half], passing.at[part, half],
            x_send.at[part, half], x_recv.at[part, half], {"vb": next_vb},
        )

    def mirror_on(part, half):
        return remote(
            passing.at[part, half], landed.at[va % ratio, half],
            m_send.at[1, part, half], m_recv.at[va % ratio, half],
            {"va": last_vb * ratio + part, "vb": va // ratio},
        )

    def mirror_passing(part, half):
        here = passing.at[part, half]
        return remote(here, here, x_send.at[part, half], x_recv.at[part, half], {"vb": vb})

    def mirror_arrival(part, half):
        here = landed.at[part, half]
        return remote(here, here, m_send.at[0, part, half], m_recv.at[part, half], {"vb": vb})

    def stays(part):
        return va == vb * ratio + part

    def last_stays(part):
        return va == last_vb * ratio + part

    def each_mirror(own, straight, out):
        for part in range(ratio):

            @pl.when(stays(part))
            def _():
                own(part)

            @pl.when(jnp.logical_not(stays(part)))
            def _():
                for half in range(halves):
                    (out if by_relay(half) else straight)(part, half)

    each_mirror(
        lambda part: mirror_own(part).start(),
        lambda part, half: mirror_straight(part, half).start(),
        lambda part, half: mirror_out(part, half).start(),
    )

    def each_passing(act):
        for part in range(ratio):

            @pl.when(jnp.logical_not(last_stays(part)))
            def _():
                for half in range(halves):
                    if by_relay(half):
                        act(part, half)

    def source(direction, step):
        return line - step if direction == 0 else line + step

    def line_slot(direction, step, chunk):
        if chunk == chunks:
            return k_slot(source(direction, step) * PAIR + 1 - side, early)
        return k_slot(source(direction, step) * PAIR + side, chunk)

    def block_at(direction, step, chunk):
        if step == 0 and chunk < chunks:
            return own_slot(chunk)
        return line_slot(direction, step, chunk)

    def line_send(direction, step, chunk):
        to = line + 1 if direction == 0 else line - 1
        return remote(
            block_at(direction, step, chunk),
            line_slot(direction, step, chunk),
            z_send.at[direction, step, chunk],
            z_recv.at[direction, step, chunk],
            {"va": to * PAIR + side},
        )

    def line_arrival(direction, step, chunk):
        here = line_slot(direction, step, chunk)
        return remote(
            here, here, z_send.at[direction, step - 1, chunk], z_recv.at[direction, step - 1, chunk],
            {"va": va},
        )

    def may_send(direction, step):
        if direction == 0:
            return jnp.logical_and(line - step >= 0, line + 1 < lines)
        return jnp.logical_and(line + step < lines, line - 1 >= 0)

    def has_arrival(direction, step):
        return line - step >= 0 if direction == 0 else line + step < lines

    def side_send(direction, step, chunk):
        return remote(
            block_at(direction, step, chunk),
            line_slot(direction, step, chunk),
            y_send.at[direction, step, chunk],
            y_recv.at[direction, step, chunk],
            {"va": line * PAIR + 1 - side},
        )

    def side_arrival(direction, step, chunk):
        here = k_slot(source(direction, step) * PAIR + 1 - side, chunk)
        return remote(
            here, here, y_send.at[direction, step, chunk], y_recv.at[direction, step, chunk], {"va": va}
        )

    def own_copy(chunk):
        return pltpu.make_async_copy(own_slot(chunk), k_slot(va, chunk), own_sem.at[ratio + 1 + chunk])

    def send_own(chunk):
        for direction in range(2):

            @pl.when(may_send(direction, 0))
            def _():
                line_send(direction, 0, chunk).start()

    side_send(0, 0, early).start()
    for chunk in range(chunks):
        send_own(chunk)
        if chunk != early:
            side_send(0, 0, chunk).start()
    for chunk in range(chunks):
        own_copy(chunk).start()
    side_arrival(0, 0, early).wait_recv()
    send_own(chunks)

    def pass_mirror(part, half):
        mirror_passing(part, half).wait_recv()
        mirror_on(part, half).start()

    each_passing(pass_mirror)

    def line_step(step):
        for chunk in range(chunks + 1):
            for direction in range(2):

                @pl.when(has_arrival(direction, step))
                def _():
                    line_arrival(direction, step, chunk).wait_recv()

                    @pl.when(may_send(direction, step))
                    def _():
                        line_send(direction, step, chunk).start()

                    if chunk < early:
                        side_send(direction, step, chunk).start()

    def spin_send(shift):
        to = lax.rem(outer + shift, outers)
        return remote(
            spin, spin_all.at[vb], s_send.at[0, shift], s_recv.at[0, shift], {"vb": to * PAIR + core}
        )

    def spin_arrival(shift):
        here = spin_all.at[lax.rem(outer + outers - shift, outers) * PAIR + core]
        return remote(here, here, s_send.at[0, shift], s_recv.at[0, shift], {"vb": vb})

    def spin_relay(shift):
        held = spin_all.at[lax.rem(outer + outers - shift, outers) * PAIR + core]
        src = spin if shift == 0 else held
        return remote(
            src, held, s_send.at[1, shift], s_recv.at[1, shift], {"vb": outer * PAIR + 1 - core}
        )

    def relay_arrival(shift):
        here = spin_all.at[lax.rem(outer + outers - shift, outers) * PAIR + 1 - core]
        return remote(here, here, s_send.at[1, shift], s_recv.at[1, shift], {"vb": vb})

    def spin_own():
        return pltpu.make_async_copy(spin, spin_all.at[vb], own_sem.at[ratio])

    def spin_step():
        for part in range(ratio):

            @pl.when(stays(part))
            def _():
                mirror_own(part).wait()

            @pl.when(jnp.logical_not(stays(part)))
            def _():
                for half in range(halves):
                    mirror_arrival(part, half).wait_recv()

            cols = slice(part * row_len, (part + 1) * row_len)
            spin[:, :, :, cols] = (
                2.0 * amp_ref[:, :, :, cols].astype(jnp.float32) - landed[part].astype(jnp.float32)
            ).astype(spin.dtype)
        for shift in range(1, outers):
            spin_send(shift).start()
        spin_relay(0).start()
        spin_own().start()

    spin_after = 1
    for step in range(1, lines):
        line_step(step)
        if step == spin_after:
            spin_step()
    if spin_after == 0:
        spin_step()
    for shift in range(1, outers):
        spin_arrival(shift).wait_recv()
        spin_relay(shift).start()

    for chunk in range(chunks + 1):
        if chunk < chunks:
            own_copy(chunk).wait()
            side_send(0, 0, chunk).wait_send()
            if chunk != early:
                side_arrival(0, 0, chunk).wait_recv()
        for direction in range(2):

            @pl.when(may_send(direction, 0))
            def _():
                line_send(direction, 0, chunk).wait_send()

    for step in range(1, lines):
        for chunk in range(chunks + 1):
            for direction in range(2):

                @pl.when(may_send(direction, step))
                def _():
                    line_send(direction, step, chunk).wait_send()

                if chunk < early:

                    @pl.when(has_arrival(direction, step))
                    def _():
                        side_arrival(direction, step, chunk).wait_recv()
                        side_send(direction, step, chunk).wait_send()

    each_mirror(
        lambda part: None,
        lambda part, half: mirror_straight(part, half).wait_send(),
        lambda part, half: mirror_out(part, half).wait_send(),
    )
    each_passing(lambda part, half: mirror_on(part, half).wait_send())

    spin_own().wait()
    for shift in range(outers):
        relay_arrival(shift).wait_recv()
        spin_relay(shift).wait_send()
    for shift in range(1, outers):
        spin_send(shift).wait_send()


def gather_all(amplitudes, turned, integrals, count_va, count_vb):
    occ_a, occ_b, row_len, col_len = amplitudes.shape
    blocks, rows, cols = integrals.shape
    chunks = blocks * SPLIT
    ratio = count_va // count_vb
    lines = count_va // PAIR
    outers = count_vb // PAIR
    dma = pltpu.SemaphoreType.DMA
    return pl.pallas_call(
        functools.partial(gather_kernel, count_va, count_vb),
        out_shape=(
            jax.ShapeDtypeStruct((blocks, count_va * rows, cols), integrals.dtype),
            jax.ShapeDtypeStruct((count_vb, occ_a, occ_b, row_len, col_len), amplitudes.dtype),
        ),
        in_specs=[pl.BlockSpec(memory_space=pltpu.VMEM)] * 3,
        out_specs=(pl.BlockSpec(memory_space=pl.ANY),) * 2,
        scratch_shapes=[
            pltpu.VMEM(turned.shape, turned.dtype),
            pltpu.VMEM(turned.shape, turned.dtype),
            pltpu.VMEM(amplitudes.shape, amplitudes.dtype),
            dma((2, lines, chunks + 1)),
            dma((2, lines, chunks + 1)),
            dma((2, lines, chunks)),
            dma((2, lines, chunks)),
            dma((2, ratio, occ_a)),
            dma((ratio, occ_a)),
            dma((ratio, occ_a)),
            dma((ratio, occ_a)),
            dma((2, outers)),
            dma((2, outers)),
            dma((ratio + 1 + chunks,)),
        ],
        compiler_params=pltpu.CompilerParams(has_side_effects=True),
    )(amplitudes, turned, integrals)


def cycle_kernel(at, screen, lengths, occ, spin_ref, k_ref, rows_ref, cols_ref, out_ref):
    slot = pl.program_id(0)
    occ_count = spin_ref.shape[1]
    row_len = out_ref.shape[2]

    @pl.when(slot == 0)
    def _():
        out_ref[...] = jnp.zeros_like(out_ref)

    @pl.when(slot < lengths[at[0]])
    def _():
        for j in range(occ_count):
            right = jnp.concatenate([k_ref[k * occ_count + j] for k in range(occ_count)], axis=0)
            for i in range(occ_count):
                left = jnp.concatenate([spin_ref[0, i, k] for k in range(occ_count)], axis=1)
                out_ref[i, j] += jnp.dot(left, right, preferred_element_type=jnp.float32)

    @pl.when(slot == pl.num_programs(0) - 1)
    def _():
        vir_rows = jnp.broadcast_to(rows_ref[0], (TILE, row_len)).T[:, :1]
        for i in range(occ_count):
            for j in range(occ_count):
                bottom = (occ[i] + occ[j] - vir_rows) - cols_ref[0]
                out_ref[i, j] = out_ref[i, j] / bottom


def local(amplitudes, integrals, occ_energy, vir_energy, screen, lengths):
    count_va = lax.axis_size("va")
    count_vb = lax.axis_size("vb")
    occ_a, occ_b, row_len, col_len = amplitudes.shape
    ratio = count_va // count_vb
    cols = integrals.shape[2]
    turned = jnp.transpose(
        amplitudes.reshape(occ_a, occ_b, row_len, ratio, row_len), (3, 0, 1, 4, 2)
    )
    whole_k, spin_all = gather_all(amplitudes, turned, integrals, count_va, count_vb)
    slots = screen.shape[1]
    per_shard = col_len // TILE
    at = jnp.stack([lax.axis_index("va"), lax.axis_index("vb")]).astype(jnp.int32)

    def tile_of(m, at, screen, lengths):
        return jnp.maximum(screen[at[0], jnp.minimum(m, lengths[at[0]] - 1)], 0)

    def spin_at(m, at, screen, lengths, occ):
        tile = tile_of(m, at, screen, lengths)
        return (tile // per_shard, 0, 0, 0, tile % per_shard)

    return pl.pallas_call(
        cycle_kernel,
        out_shape=jax.ShapeDtypeStruct((occ_a, occ_b, row_len, cols), jnp.float32),
        grid_spec=pltpu.PrefetchScalarGridSpec(
            num_scalar_prefetch=4,
            grid=(slots,),
            in_specs=[
                pl.BlockSpec((1, occ_a, occ_b, row_len, TILE), spin_at),
                pl.BlockSpec(
                    (integrals.shape[0], TILE, cols),
                    lambda m, at, screen, lengths, occ: (0, tile_of(m, at, screen, lengths), 0),
                ),
                pl.BlockSpec((1, 1, row_len), lambda m, at, screen, lengths, occ: (at[0], 0, 0)),
                pl.BlockSpec((1, 1, cols), lambda m, at, screen, lengths, occ: (at[1], 0, 0)),
            ],
            out_specs=pl.BlockSpec(
                (occ_a, occ_b, row_len, cols), lambda m, at, screen, lengths, occ: (0, 0, 0, 0)
            ),
        ),
    )(
        at, screen, lengths, occ_energy, spin_all, whole_k,
        vir_energy.reshape(count_va, 1, row_len), vir_energy.reshape(count_vb, 1, cols),
    )


def solution(mesh):
    return jax.shard_map(
        local,
        mesh=mesh,
        in_specs=(P(None, None, "va", "vb"), P(None, "va", "vb"), P(), P(), P(), P()),
        out_specs=P(None, None, "va", "vb"),
        check_vma=False,
    )
```

```python
import functools

import jax
import jax.numpy as jnp
from jax import lax
from jax.experimental import pallas as pl
from jax.experimental.pallas import tpu as pltpu
from jax.sharding import PartitionSpec as P

TILE = 128
PAIR = 2
SPLIT = 2
GROUP = 2
MESH = pl.DeviceIdType.MESH


def gather_kernel(
    count_va, count_vb, flip, amp_ref, *refs
):
    refs = list(refs)
    turned_ref = None if flip else refs.pop(0)
    (
        int_ref, whole_k, spin_all,
        landed, passing, spin, z_send, z_recv, y_send, y_recv, m_send, m_recv, x_send, x_recv, s_send, s_recv, own_sem,
    ) = refs
    va = lax.axis_index("va")
    vb = lax.axis_index("vb")
    ratio = count_va // count_vb
    lines = count_va // PAIR
    outers = count_vb // PAIR
    line, side = va // PAIR, va % PAIR
    outer, core = vb // PAIR, vb % PAIR
    blocks, rows, _ = int_ref.shape
    part_rows = rows // SPLIT
    chunks = blocks * SPLIT
    early = chunks - 1
    halves = amp_ref.shape[0]
    row_len = amp_ref.shape[2]

    def k_slot(owner, chunk):
        begin = owner * rows + chunk % SPLIT * part_rows
        return whole_k.at[chunk // SPLIT, pl.ds(pl.multiple_of(begin, part_rows), part_rows)]

    def own_slot(chunk):
        return int_ref.at[chunk // SPLIT, pl.ds(chunk % SPLIT * part_rows, part_rows)]

    def remote(src, dst, send, recv, target):
        return pltpu.make_async_remote_copy(
            src_ref=src, dst_ref=dst, send_sem=send, recv_sem=recv, device_id=target, device_id_type=MESH
        )

    next_vb = lax.rem(outer + 1, outers) * PAIR + core
    last_vb = lax.rem(outer + outers - 1, outers) * PAIR + core

    def by_relay(half):
        return outers > 1 and half % 2 == 1

    def piece(part):
        if flip:
            return amp_ref.at[:, :, :, pl.ds(part * row_len, row_len)]
        return turned_ref.at[part]

    def half_piece(part, half):
        if flip:
            return amp_ref.at[half, :, :, pl.ds(part * row_len, row_len)]
        return turned_ref.at[part, half]

    def mirror_own(part):
        return pltpu.make_async_copy(piece(part), landed.at[part], own_sem.at[part])

    def mirror_straight(part, half):
        return remote(
            half_piece(part, half), landed.at[va % ratio, half],
            m_send.at[0, part, half], m_recv.at[va % ratio, half],
            {"va": vb * ratio + part, "vb": va // ratio},
        )

    def mirror_out(part, half):
        return remote(
            half_piece(part, half), passing.at[part, half],
            x_send.at[part, half], x_recv.at[part, half], {"vb": next_vb},
        )

    def mirror_on(part, half):
        return remote(
            passing.at[part, half], landed.at[va % ratio, half],
            m_send.at[1, part, half], m_recv.at[va % ratio, half],
            {"va": last_vb * ratio + part, "vb": va // ratio},
        )

    def mirror_passing(part, half):
        here = passing.at[part, half]
        return remote(here, here, x_send.at[part, half], x_recv.at[part, half], {"vb": vb})

    def mirror_arrival(part, half):
        here = landed.at[part, half]
        return remote(here, here, m_send.at[0, part, half], m_recv.at[part, half], {"vb": vb})

    def stays(part):
        return va == vb * ratio + part

    def last_stays(part):
        return va == last_vb * ratio + part

    def each_mirror(own, straight, out):
        for part in range(ratio):

            @pl.when(stays(part))
            def _():
                own(part)

            @pl.when(jnp.logical_not(stays(part)))
            def _():
                for half in range(halves):
                    (out if by_relay(half) else straight)(part, half)

    each_mirror(
        lambda part: mirror_own(part).start(),
        lambda part, half: mirror_straight(part, half).start(),
        lambda part, half: mirror_out(part, half).start(),
    )

    def each_passing(act):
        for part in range(ratio):

            @pl.when(jnp.logical_not(last_stays(part)))
            def _():
                for half in range(halves):
                    if by_relay(half):
                        act(part, half)

    def source(direction, step):
        return line - step if direction == 0 else line + step

    def line_slot(direction, step, chunk):
        if chunk == chunks:
            return k_slot(source(direction, step) * PAIR + 1 - side, early)
        return k_slot(source(direction, step) * PAIR + side, chunk)

    def block_at(direction, step, chunk):
        if step == 0 and chunk < chunks:
            return own_slot(chunk)
        return line_slot(direction, step, chunk)

    def line_send(direction, step, chunk):
        to = line + 1 if direction == 0 else line - 1
        return remote(
            block_at(direction, step, chunk),
            line_slot(direction, step, chunk),
            z_send.at[direction, step, chunk],
            z_recv.at[direction, step, chunk],
            {"va": to * PAIR + side},
        )

    def line_arrival(direction, step, chunk):
        here = line_slot(direction, step, chunk)
        return remote(
            here, here, z_send.at[direction, step - 1, chunk], z_recv.at[direction, step - 1, chunk],
            {"va": va},
        )

    def may_send(direction, step):
        if direction == 0:
            return jnp.logical_and(line - step >= 0, line + 1 < lines)
        return jnp.logical_and(line + step < lines, line - 1 >= 0)

    def has_arrival(direction, step):
        return line - step >= 0 if direction == 0 else line + step < lines

    def side_send(direction, step, chunk):
        return remote(
            block_at(direction, step, chunk),
            line_slot(direction, step, chunk),
            y_send.at[direction, step, chunk],
            y_recv.at[direction, step, chunk],
            {"va": line * PAIR + 1 - side},
        )

    def side_arrival(direction, step, chunk):
        here = k_slot(source(direction, step) * PAIR + 1 - side, chunk)
        return remote(
            here, here, y_send.at[direction, step, chunk], y_recv.at[direction, step, chunk], {"va": va}
        )

    def own_copy(chunk):
        return pltpu.make_async_copy(own_slot(chunk), k_slot(va, chunk), own_sem.at[ratio + 1 + chunk])

    def send_own(chunk):
        for direction in range(2):

            @pl.when(may_send(direction, 0))
            def _():
                line_send(direction, 0, chunk).start()

    side_send(0, 0, early).start()
    for chunk in range(chunks):
        send_own(chunk)
        if chunk != early:
            side_send(0, 0, chunk).start()
    for chunk in range(chunks):
        own_copy(chunk).start()
    side_arrival(0, 0, early).wait_recv()
    send_own(chunks)

    def pass_mirror(part, half):
        mirror_passing(part, half).wait_recv()
        mirror_on(part, half).start()

    each_passing(pass_mirror)

    def line_step(step):
        for chunk in range(chunks + 1):
            for direction in range(2):

                @pl.when(has_arrival(direction, step))
                def _():
                    line_arrival(direction, step, chunk).wait_recv()

                    @pl.when(may_send(direction, step))
                    def _():
                        line_send(direction, step, chunk).start()

                    if chunk < early:
                        side_send(direction, step, chunk).start()

    def spin_send(shift):
        to = lax.rem(outer + shift, outers)
        return remote(
            spin, spin_all.at[vb], s_send.at[0, shift], s_recv.at[0, shift], {"vb": to * PAIR + core}
        )

    def spin_arrival(shift):
        here = spin_all.at[lax.rem(outer + outers - shift, outers) * PAIR + core]
        return remote(here, here, s_send.at[0, shift], s_recv.at[0, shift], {"vb": vb})

    def spin_relay(shift):
        held = spin_all.at[lax.rem(outer + outers - shift, outers) * PAIR + core]
        src = spin if shift == 0 else held
        return remote(
            src, held, s_send.at[1, shift], s_recv.at[1, shift], {"vb": outer * PAIR + 1 - core}
        )

    def relay_arrival(shift):
        here = spin_all.at[lax.rem(outer + outers - shift, outers) * PAIR + 1 - core]
        return remote(here, here, s_send.at[1, shift], s_recv.at[1, shift], {"vb": vb})

    def spin_own():
        return pltpu.make_async_copy(spin, spin_all.at[vb], own_sem.at[ratio])

    def spin_step():
        for part in range(ratio):

            @pl.when(stays(part))
            def _():
                mirror_own(part).wait()

            @pl.when(jnp.logical_not(stays(part)))
            def _():
                for half in range(halves):
                    mirror_arrival(part, half).wait_recv()

            cols = slice(part * row_len, (part + 1) * row_len)
            for i in range(halves):
                for k in range(amp_ref.shape[1]):
                    mirror = landed[part, i, k].astype(jnp.float32)
                    spin[i, k, :, cols] = (
                        2.0 * amp_ref[i, k, :, cols].astype(jnp.float32) - (mirror.T if flip else mirror)
                    ).astype(spin.dtype)
        for shift in range(1, outers):
            spin_send(shift).start()
        spin_relay(0).start()
        spin_own().start()

    spin_after = 1
    for step in range(1, lines):
        line_step(step)
        if step == spin_after:
            spin_step()
    if spin_after == 0:
        spin_step()
    for shift in range(1, outers):
        spin_arrival(shift).wait_recv()
        spin_relay(shift).start()

    for chunk in range(chunks + 1):
        if chunk < chunks:
            own_copy(chunk).wait()
            side_send(0, 0, chunk).wait_send()
            if chunk != early:
                side_arrival(0, 0, chunk).wait_recv()
        for direction in range(2):

            @pl.when(may_send(direction, 0))
            def _():
                line_send(direction, 0, chunk).wait_send()

    for step in range(1, lines):
        for chunk in range(chunks + 1):
            for direction in range(2):

                @pl.when(may_send(direction, step))
                def _():
                    line_send(direction, step, chunk).wait_send()

                if chunk < early:

                    @pl.when(has_arrival(direction, step))
                    def _():
                        side_arrival(direction, step, chunk).wait_recv()
                        side_send(direction, step, chunk).wait_send()

    each_mirror(
        lambda part: None,
        lambda part, half: mirror_straight(part, half).wait_send(),
        lambda part, half: mirror_out(part, half).wait_send(),
    )
    each_passing(lambda part, half: mirror_on(part, half).wait_send())

    spin_own().wait()
    for shift in range(outers):
        relay_arrival(shift).wait_recv()
        spin_relay(shift).wait_send()
    for shift in range(1, outers):
        spin_send(shift).wait_send()


def gather_all(amplitudes, integrals, count_va, count_vb):
    occ_a, occ_b, row_len, col_len = amplitudes.shape
    blocks, rows, cols = integrals.shape
    chunks = blocks * SPLIT
    ratio = count_va // count_vb
    lines = count_va // PAIR
    outers = count_vb // PAIR
    flip = row_len % TILE == 0
    operands = (amplitudes, integrals)
    if not flip:
        turned = amplitudes.reshape(occ_a, occ_b, row_len, ratio, row_len)
        operands = (amplitudes, jnp.transpose(turned, (3, 0, 1, 4, 2)), integrals)
    mirror_shape = (ratio, occ_a, occ_b, row_len, row_len)
    dma = pltpu.SemaphoreType.DMA
    return pl.pallas_call(
        functools.partial(gather_kernel, count_va, count_vb, flip),
        out_shape=(
            jax.ShapeDtypeStruct((blocks, count_va * rows, cols), integrals.dtype),
            jax.ShapeDtypeStruct((count_vb, occ_a, occ_b, row_len, col_len), amplitudes.dtype),
        ),
        in_specs=[pl.BlockSpec(memory_space=pltpu.VMEM)] * len(operands),
        out_specs=(pl.BlockSpec(memory_space=pl.ANY),) * 2,
        scratch_shapes=[
            pltpu.VMEM(mirror_shape, amplitudes.dtype),
            pltpu.VMEM(mirror_shape, amplitudes.dtype),
            pltpu.VMEM(amplitudes.shape, amplitudes.dtype),
            dma((2, lines, chunks + 1)),
            dma((2, lines, chunks + 1)),
            dma((2, lines, chunks)),
            dma((2, lines, chunks)),
            dma((2, ratio, occ_a)),
            dma((ratio, occ_a)),
            dma((ratio, occ_a)),
            dma((ratio, occ_a)),
            dma((2, outers)),
            dma((2, outers)),
            dma((ratio + 1 + chunks,)),
        ],
        compiler_params=pltpu.CompilerParams(has_side_effects=True),
    )(*operands)


def cycle_kernel(at, screen, lengths, occ, *refs):
    spin_refs, k_refs = refs[:GROUP], refs[GROUP : 2 * GROUP]
    rows_ref, cols_ref, out_ref = refs[2 * GROUP :]
    slot = pl.program_id(0) * GROUP
    occ_count = out_ref.shape[0]
    count = lengths[at[0]]
    row_len = out_ref.shape[2]

    @pl.when(slot == 0)
    def _():
        out_ref[...] = jnp.zeros_like(out_ref)

    @pl.when(slot < count)
    def _():
        pairs = [(m, k) for m in range(GROUP) for k in range(occ_count)]
        live = [(slot + m < count).astype(spin_refs[0].dtype) for m in range(GROUP)]
        lefts = [
            jnp.concatenate([spin_refs[m][0, i, k] * live[m] for m, k in pairs], axis=1)
            for i in range(occ_count)
        ]
        for j in range(occ_count):
            right = jnp.concatenate([k_refs[m][k * occ_count + j] for m, k in pairs], axis=0)
            for i in range(occ_count):
                out_ref[i, j] += jnp.dot(lefts[i], right, preferred_element_type=jnp.float32)

    @pl.when(pl.program_id(0) == pl.num_programs(0) - 1)
    def _():
        vir_rows = jnp.broadcast_to(rows_ref[0], (TILE, row_len)).T[:, :1]
        for i in range(occ_count):
            for j in range(occ_count):
                bottom = (occ[i] + occ[j] - vir_rows) - cols_ref[0]
                out_ref[i, j] = out_ref[i, j] / bottom


def local(amplitudes, integrals, occ_energy, vir_energy, screen, lengths):
    count_va = lax.axis_size("va")
    count_vb = lax.axis_size("vb")
    occ_a, occ_b, row_len, col_len = amplitudes.shape
    cols = integrals.shape[2]
    whole_k, spin_all = gather_all(amplitudes, integrals, count_va, count_vb)
    slots = screen.shape[1]
    per_shard = col_len // TILE
    at = jnp.stack([lax.axis_index("va"), lax.axis_index("vb")]).astype(jnp.int32)

    def tile_of(m, at, screen, lengths):
        return jnp.maximum(screen[at[0], jnp.minimum(m, lengths[at[0]] - 1)], 0)

    def spin_at(place, m, at, screen, lengths, occ):
        tile = tile_of(m * GROUP + place, at, screen, lengths)
        return (tile // per_shard, 0, 0, 0, tile % per_shard)

    def k_at(place, m, at, screen, lengths, occ):
        return (0, tile_of(m * GROUP + place, at, screen, lengths), 0)

    return pl.pallas_call(
        cycle_kernel,
        out_shape=jax.ShapeDtypeStruct((occ_a, occ_b, row_len, cols), jnp.float32),
        grid_spec=pltpu.PrefetchScalarGridSpec(
            num_scalar_prefetch=4,
            grid=(pl.cdiv(slots, GROUP),),
            in_specs=[
                *(
                    pl.BlockSpec((1, occ_a, occ_b, row_len, TILE), functools.partial(spin_at, place))
                    for place in range(GROUP)
                ),
                *(
                    pl.BlockSpec((integrals.shape[0], TILE, cols), functools.partial(k_at, place))
                    for place in range(GROUP)
                ),
                pl.BlockSpec((1, 1, row_len), lambda m, at, screen, lengths, occ: (at[0], 0, 0)),
                pl.BlockSpec((1, 1, cols), lambda m, at, screen, lengths, occ: (at[1], 0, 0)),
            ],
            out_specs=pl.BlockSpec(
                (occ_a, occ_b, row_len, cols), lambda m, at, screen, lengths, occ: (0, 0, 0, 0)
            ),
        ),
    )(
        at, screen, lengths, occ_energy, *[spin_all] * GROUP, *[whole_k] * GROUP,
        vir_energy.reshape(count_va, 1, row_len), vir_energy.reshape(count_vb, 1, cols),
    )


def solution(mesh):
    return jax.shard_map(
        local,
        mesh=mesh,
        in_specs=(P(None, None, "va", "vb"), P(None, "va", "vb"), P(), P(), P(), P()),
        out_specs=P(None, None, "va", "vb"),
        check_vma=False,
    )
```
